32 devices in a mesh: band: 4 (over z), strip: 8 (over y, x, core).
Axes of the slice: x: 2, y: 2, z: 4, core: 2. Of those that a mesh axis runs over, the one named last changes fastest.
Arguments:
- first_scene: bfloat16 [2048, 4096], P('band', 'strip'), may hold values from -6 to 6
- second_scene: bfloat16 [2048, 4096], P('band', 'strip'), may hold values from -6 to 6
- owner_strip: int32 [4, 8, 16, 1], P('band', 'strip'), may hold values from 0 to 7; in each aligned block of 16 rows (0 to 15, 16 to 31, ..., all dimensions but the last counted through in order) at most 4 rows name the same one
- target_tile: int32 [4, 8, 16], P('band', 'strip'), may hold values from 0 to 15
- offsets: int32 [4, 8, 16, 2], P('band', 'strip'), may hold values from -32 to 32
- valid_mask: int32 [4, 8, 16], P('band', 'strip'), may hold values 0 or 1
Outputs:
- consistency: float32 [4, 8, 16, 4096], P('band', 'strip')
The draws below stay inside these ranges and needn't reach their ends.
Inputs may be any that keep to these rules, and one draw needn't show every extreme that they name: `owner_strip`: among the 16 patches of one device at most 4 name the same owner strip, and in every draw some device has 4 patches naming one strip.
All inputs are finite; a program needn't handle non-finite values. No bound on the sum of `valid_mask` on one device may be relied on, other than what follows from the above.
Results may differ from the reference program's by a relative error of at most 0.0003.
Values may be sent and summed in bfloat16 or wider, within the bound.
A program may use at most 128 MiB of HBM per device.

```python
import math
import jax
import jax.numpy as jnp
import numpy as np
from jax import lax

PATCH_SIDE = 128
SHIFTS = 64
ROW_PATCHES = 4
COL_PATCHES = 4
PATCHES = 16
SEARCH = 192
PADDED = 256
CAPACITY = 4
IMAGE_ROWS = 2048
IMAGE_COLS = 4096
N_BAND = 4
N_STRIP = 8


def place_ends(result, own_key, least, top_value):
    dims = result.shape
    spot = [jax.random.randint(jax.random.fold_in(own_key, axis), (), 0, dims[axis]) for axis in range(len(dims))]
    result = result.at[tuple(spot)].set(least)
    longest = dims.index(max(dims))
    spot[longest] = (spot[longest] + 1) % dims[longest]
    return result.at[tuple(spot)].set(top_value)


def block_scale(key, extent, pieces, low, high):
    def one(position, shards_of):
        steps = jax.random.uniform(jax.random.fold_in(jax.random.fold_in(key, 6), position), (shards_of,), jnp.float32, low / len(pieces), high / len(pieces))
        return jnp.repeat(jnp.exp(steps), extent[position] // shards_of).reshape((-1,) + (1,) * (len(extent) - position - 1))

    level = one(*pieces[0])
    for cut in pieces[1:]:
        level = level * one(*cut)
    return level


def assign_block(key, own, number, rows, number_of, top, limit, lean):
    sequence = jax.random.permutation(key, number_of)
    packed, usual = portions_of(number_of, rows * top, limit, lean, True), portions_of(number_of, rows * top, limit, lean, False)
    places = jnp.arange(number_of)

    def named(tallies, turn):
        used = int((tallies > 0).sum())
        fixed = max(1, used // 4)
        passed = fixed + (places - fixed + turn * (used - fixed)) % max(1, number_of - fixed)
        return jnp.zeros((number_of,), jnp.int32).at[sequence[jnp.where(places < fixed, places, passed)]].set(jnp.asarray(tallies, jnp.int32))

    tallies = jnp.where(number % 4 == 0, named(packed, number // 4), named(usual, number - number // 4 - 1))
    mixed = jax.random.permutation(jax.random.fold_in(own, 3), number_of)
    giver, receiver = mixed[0:number_of // 2 * 2:2], mixed[1:number_of // 2 * 2:2]
    margin = jnp.minimum(tallies[giver] - 1, limit - tallies[receiver]) // 2
    margin = jnp.where((giver == sequence[0]) | (receiver == sequence[0]) | (tallies[receiver] == 0), 0, jnp.maximum(margin, 0))
    passed = jax.random.randint(jax.random.fold_in(own, 4), (number_of // 2,), 0, 1 << 20) % (margin + 1)
    tallies = tallies.at[giver].add(-passed).at[receiver].add(passed)
    labels = jnp.searchsorted(jnp.cumsum(tallies), jnp.arange(rows * top), side="right").astype(jnp.int32)
    listing = labels.reshape(top, rows).T
    listing = listing[jax.random.permutation(jax.random.fold_in(own, 1), rows)]
    turn = jax.random.randint(jax.random.fold_in(own, 2), (rows, 1), 0, top)
    return jnp.take_along_axis(listing, (jnp.arange(top)[None, :] + turn) % top, axis=1)


def portions_of(number_of, total, bound, slope, full):
    weights = [(1 << 20) // math.isqrt(standing ** slope) + 1 for standing in range(1, number_of + 1)]
    largest = bound if full else min(bound, max(-(-total // number_of), total * weights[0] // sum(weights)))
    least = 1 if total - largest >= number_of - 1 else 0
    given, spare = [largest] + [least] * (number_of - 1), total - largest - least * (number_of - 1)
    while spare > 0:
        movable = [i for i in range(1, number_of) if given[i] < largest] or [i for i in range(1, number_of) if given[i] < bound]
        whole, remaining = sum([weights[i] for i in movable]), spare
        for i in movable:
            more = min(bound - given[i], max(1, remaining * weights[i] // whole), spare)
            given[i] = given[i] + more
            spare = spare - more
    return np.array(given)


def noise(key, shape, spread, bound, pieces=(), held_as=jnp.bfloat16):
    gain = block_scale(key, shape, pieces, -0.22, 0.18) if pieces else 1.0
    values = jax.random.normal(key, shape, jnp.float32) * spread * gain
    return jnp.minimum(jnp.maximum(values, -bound), bound).astype(held_as)


def setup_inputs(seed: int = 0) -> dict:
    key_list = jax.random.split(jax.random.key(seed), 7)
    first_scene = noise(key_list[0], (IMAGE_ROWS, IMAGE_COLS), 1.0, 6.0, ((0, 4), (1, 8)))
    second_scene = noise(key_list[1], (IMAGE_ROWS, IMAGE_COLS), 1.0, 6.0, ((0, 4), (1, 8)))
    owner_strip_keys = jax.random.split(jax.random.fold_in(key_list[2], 1), N_BAND * N_STRIP * PATCHES // PATCHES)
    owner_strip_turns = jax.random.permutation(jax.random.fold_in(key_list[2], 3), N_BAND * N_STRIP * PATCHES // PATCHES)
    owner_strip = jax.vmap(lambda own, number: assign_block(jax.random.fold_in(key_list[2], 2), own, number, PATCHES, N_STRIP, 1, CAPACITY, 2))(owner_strip_keys, owner_strip_turns).reshape((N_BAND, N_STRIP, PATCHES, 1))
    target_tile = place_ends(jax.random.randint(key_list[3], (N_BAND, N_STRIP, PATCHES), 0, PATCHES), jax.random.fold_in(key_list[3], 1), 0, PATCHES - 1).astype(jnp.int32)
    offsets = place_ends(jax.random.randint(key_list[4], (N_BAND, N_STRIP, PATCHES, 2), 0 - SHIFTS // 2, SHIFTS // 2 + 1), jax.random.fold_in(key_list[4], 1), 0 - SHIFTS // 2, (SHIFTS // 2 + 1) - 1).astype(jnp.int32)
    valid_mask = place_ends((jax.random.randint(key_list[5], (N_BAND, N_STRIP, PATCHES), 0, 4) < 3).astype(jnp.int32), jax.random.fold_in(key_list[5], 1), 0, 1)
    return dict(first_scene=first_scene, second_scene=second_scene, owner_strip=owner_strip, target_tile=target_tile, offsets=offsets, valid_mask=valid_mask)


EPSILON = 1e-05

def normalize(patch):
    centered = patch - jnp.mean(patch)
    return centered * lax.rsqrt(jnp.mean(centered * centered) + EPSILON)

def correlate(template, window):
    spec_template = jnp.fft.rfft2(template, s=(PADDED, PADDED))
    spec_window = jnp.fft.rfft2(window, s=(PADDED, PADDED))
    surface = jnp.fft.irfft2(jnp.conj(spec_template) * spec_window, s=(PADDED, PADDED))
    return surface[:SHIFTS, :SHIFTS]

def reference(first_scene, second_scene, owner_strip, target_tile, offsets, valid_mask):
    middle = SHIFTS // 2
    padded_first = jnp.pad(first_scene, SHIFTS)
    padded_second = jnp.pad(second_scene, SHIFTS)
    patch_total = N_BAND * N_STRIP * PATCHES
    owners = owner_strip.reshape(patch_total).astype(jnp.int32)
    tile_list = target_tile.reshape(patch_total).astype(jnp.int32)
    shifts = offsets.reshape(patch_total, 2).astype(jnp.int32)
    mask_list = valid_mask.reshape(patch_total)
    indices = jnp.arange(patch_total, dtype=jnp.int32)

    def one_patch(inputs):
        patch_index, strip_owner, tile_index, fine_shift, keep_flag = inputs
        band_index = patch_index // (N_STRIP * PATCHES)
        strip_index = patch_index // PATCHES % N_STRIP
        local_index = patch_index % PATCHES
        patch_top = (band_index * ROW_PATCHES + local_index // COL_PATCHES) * PATCH_SIDE
        patch_left = (strip_index * COL_PATCHES + local_index % COL_PATCHES) * PATCH_SIDE
        target_top = (band_index * ROW_PATCHES + tile_index // COL_PATCHES) * PATCH_SIDE
        target_left = (strip_owner * COL_PATCHES + tile_index % COL_PATCHES) * PATCH_SIDE
        search = lax.dynamic_slice(padded_second, ((target_top + fine_shift[0] - middle + SHIFTS).astype(jnp.int32), (target_left + fine_shift[1] - middle + SHIFTS).astype(jnp.int32)), (SEARCH, SEARCH)).astype(jnp.float32)
        beside_all = lax.dynamic_slice(padded_first, ((patch_top - middle + 1 + SHIFTS).astype(jnp.int32), (patch_left - middle + 1 + SHIFTS).astype(jnp.int32)), (SEARCH, SEARCH)).astype(jnp.float32)
        template = normalize(beside_all[middle - 1:middle - 1 + PATCH_SIDE, middle - 1:middle - 1 + PATCH_SIDE])
        backward = normalize(search[middle:middle + PATCH_SIDE, middle:middle + PATCH_SIDE])
        forward_surface = correlate(template, search)
        backward_surface = correlate(backward, beside_all)
        combined = (forward_surface + backward_surface[::-1, ::-1]) / (2.0 * PATCH_SIDE)
        return (combined * keep_flag.astype(jnp.float32)).reshape(SHIFTS * SHIFTS)
    surfaces = lax.map(one_patch, (indices, owners, tile_list, shifts, mask_list))
    return surfaces.reshape(N_BAND, N_STRIP, PATCHES, SHIFTS * SHIFTS)
```

```python
import functools

import jax
import jax.numpy as jnp
from jax import lax
from jax.experimental import pallas as pl
from jax.experimental.pallas import tpu as pltpu
from jax.sharding import PartitionSpec as P

PATCH_SIDE = 128
SHIFTS = 64
SEARCH = 192
WIDE = 256
LANES = 128
HALO = 64
EPSILON = 1e-05
GROUPS = 16
STEP = SEARCH // GROUPS
CHUNK = 16
HIGHEST = lax.Precision.HIGHEST
NT = (((1,), (1,)), ((), ()))


def iota(shape, dim):
    return lax.broadcasted_iota(jnp.int32, shape, dim)


def onehot(mask):
    return jnp.where(mask, 1.0, 0.0).astype(jnp.bfloat16)


def cut(raw, row_start, col_start, row_inner, col_inner, low, high):
    row_id = iota((SEARCH, WIDE), 0)
    source = row_start + STEP * (GROUPS - 1 - row_id % GROUPS) + row_id // GROUPS
    take_rows = onehot(iota((SEARCH, WIDE), 1) == source)
    inner_id = iota((WIDE + 16, WIDE), 0) - (SHIFTS - 1)
    inside = (inner_id >= 0) & (inner_id < PATCH_SIDE)
    take_inner = onehot(
        (iota((WIDE + 16, WIDE), 1) == row_start + row_inner + inner_id) & inside
    )
    rows = jnp.dot(
        jnp.concatenate([take_rows, take_inner], axis=0), raw, preferred_element_type=jnp.float32
    ).astype(jnp.bfloat16)
    from_col = iota((3 * LANES, WIDE), 0)
    to_col = iota((3 * LANES, WIDE), 1)
    real = (from_col >= low) & (from_col < high)
    take_cols = onehot((from_col == to_col + col_start) & (to_col < SEARCH) & real)
    window = jnp.dot(rows[:SEARCH], take_cols, preferred_element_type=jnp.float32)
    from_col = iota((3 * LANES, LANES), 0)
    real = (from_col >= low) & (from_col < high)
    take_cols = onehot(
        (from_col == iota((3 * LANES, LANES), 1) + col_start + col_inner) & real
    )
    inner = jnp.dot(rows[SEARCH:], take_cols, preferred_element_type=jnp.float32)
    return window, inner


def correlate(window, inner, inner_ref, weight_ref, shift_ref, reverse):
    inner_ref[...] = inner
    for i in range(STEP):
        weight_ref[:, i * LANES : (i + 1) * LANES] = inner_ref[i : i + WIDE, :].astype(jnp.bfloat16)
    count = PATCH_SIDE * PATCH_SIDE
    patch = inner_ref[SHIFTS - 1 : SHIFTS - 1 + PATCH_SIDE, :]
    mean = jnp.sum(patch) / count
    centered = patch - mean
    gain = lax.rsqrt(jnp.full((1, LANES), jnp.sum(centered * centered) / count + EPSILON))

    lane = iota((SEARCH, LANES), 1)
    left, right = window[:, :LANES], window[:, LANES:]
    parts = []
    for first in range(0, SHIFTS, CHUNK):
        for slot in range(first, first + CHUNK):
            shift = SHIFTS - 1 - slot if reverse else slot
            if shift:
                moved = pltpu.roll(jnp.where(lane < shift, right, left), LANES - shift, 1)
            else:
                moved = left
            moved = moved.astype(jnp.bfloat16)
            for i in range(STEP):
                shift_ref[slot * GROUPS : (slot + 1) * GROUPS, i * LANES : (i + 1) * LANES] = moved[
                    i * GROUPS : (i + 1) * GROUPS
                ]
        product = lax.dot_general(
            shift_ref[first * GROUPS : (first + CHUNK) * GROUPS, :],
            weight_ref[...],
            NT,
            preferred_element_type=jnp.float32,
        )
        for k in range(CHUNK):
            rows = product[k * GROUPS : (k + 1) * GROUPS]
            half = GROUPS // 2
            rows = rows[:half] + pltpu.roll(rows[half:], STEP * half, 1)
            skewed = pltpu.roll(rows, 0, 1, stride=STEP, stride_axis=0)
            parts.append(jnp.sum(skewed, axis=0, keepdims=True))
    raw = jnp.concatenate(parts, axis=0)
    raw = pltpu.roll(raw, WIDE - STEP * (GROUPS - 1), 1)[:, :LANES]

    slot = iota((SHIFTS, WIDE), 0)
    v = SHIFTS - 1 - slot if reverse else slot
    col = iota((SHIFTS, WIDE), 1)
    across = lax.dot_general(
        onehot((col >= v) & (col < v + PATCH_SIDE)),
        window.astype(jnp.bfloat16),
        NT,
        preferred_element_type=jnp.float32,
    )
    row_id = iota((SEARCH, LANES), 0)
    row = STEP * (GROUPS - 1 - row_id % GROUPS) + row_id // GROUPS
    u = SHIFTS - 1 - lane
    down = jnp.where((row >= u) & (row < u + PATCH_SIDE), 1.0, 0.0)
    sums = jnp.dot(across, down, precision=HIGHEST, preferred_element_type=jnp.float32)
    return gain * (raw - mean * sums)


def kernel(per_row, tiles, owner, tile, offset, valid, *refs):
    first, second = refs[:6], refs[6:12]
    out_ref, inner_ref, weight_ref, shift_ref = refs[12:]
    k = pl.program_id(0)
    middle = SHIFTS // 2

    def gathered(blocks):
        return jnp.concatenate(
            [
                jnp.concatenate([blocks[3 * r + c][...].reshape(LANES, LANES) for c in range(3)], axis=1)
                for r in range(2)
            ],
            axis=0,
        )

    around = cut(
        gathered(first), HALO - middle + 1, LANES - middle + 1, middle - 1, middle - 1, 0, 3 * LANES
    )
    place = owner[k] * per_row + tile[k] % per_row
    low = jnp.where(place == 0, LANES, 0)
    high = jnp.where(place == tiles - 1, 2 * LANES, 3 * LANES)
    search = cut(
        gathered(second),
        HALO - middle + offset[2 * k],
        LANES - middle + offset[2 * k + 1],
        middle,
        middle,
        low,
        high,
    )
    ahead = correlate(search[0], around[1], inner_ref, weight_ref, shift_ref, False)
    behind = correlate(around[0], search[1], inner_ref, weight_ref, shift_ref, True)
    lane = iota((SHIFTS, LANES), 1)
    both = jnp.where(lane < SHIFTS, ahead, pltpu.roll(behind, SHIFTS, 1))
    u = iota((SHIFTS, LANES), 0)
    pick = jnp.where((lane == SHIFTS - 1 - u) | (lane == SHIFTS + u), 1.0, 0.0)
    surface = lax.dot_general(
        pick, both, NT, precision=HIGHEST, preferred_element_type=jnp.float32
    )
    scale = valid[k].astype(jnp.float32) / (2.0 * PATCH_SIDE)
    out_ref[0] = surface * scale


def surfaces(first, gathered, owner, tile, offset, valid):
    strips = gathered.shape[0]
    per_row = gathered.shape[2] // LANES
    tiles = strips * per_row
    patch_count = owner.shape[0]

    def first_spec(r, c):
        return pl.BlockSpec((LANES, LANES), lambda k, *_: (k // per_row + r, k % per_row + c))

    def second_spec(r, c):
        def index(k, owner, tile, offset, valid):
            place = owner[k] * per_row + tile[k] % per_row + (c - 1)
            place = jnp.minimum(jnp.maximum(place, 0), tiles - 1)
            return (place // per_row, tile[k] // per_row + r, place % per_row)

        return pl.BlockSpec((1, LANES, LANES), index)

    cells = [(r, c) for r in range(2) for c in range(3)]
    return pl.pallas_call(
        functools.partial(kernel, per_row, tiles),
        out_shape=jax.ShapeDtypeStruct((patch_count, SHIFTS, SHIFTS), jnp.float32),
        grid_spec=pltpu.PrefetchScalarGridSpec(
            num_scalar_prefetch=4,
            grid=(patch_count,),
            in_specs=[first_spec(*cell) for cell in cells] + [second_spec(*cell) for cell in cells],
            out_specs=pl.BlockSpec((1, SHIFTS, SHIFTS), lambda k, *_: (k, 0, 0)),
            scratch_shapes=[
                pltpu.VMEM((WIDE + 16, LANES), jnp.float32),
                pltpu.VMEM((WIDE, STEP * LANES), jnp.bfloat16),
                pltpu.VMEM((SHIFTS * GROUPS, STEP * LANES), jnp.bfloat16),
            ],
        ),
    )(owner, tile, offset, valid, *([first] * 6), *([gathered] * 6))


def both_ways(axis, tail, head):
    count = lax.axis_size(axis)
    before = lax.ppermute(tail, axis, [(i, i + 1) for i in range(count - 1)])
    after = lax.ppermute(head, axis, [(i + 1, i) for i in range(count - 1)])
    return before, after


def on_device(first_scene, second_scene, owner_strip, target_tile, offsets, valid_mask):
    per_row = first_scene.shape[1] // PATCH_SIDE
    patch_count = first_scene.shape[0] // PATCH_SIDE * per_row
    above, below = both_ways(
        "band",
        jnp.concatenate([first_scene[-HALO:], second_scene[-HALO:]], axis=0),
        jnp.concatenate([first_scene[:HALO], second_scene[:HALO]], axis=0),
    )
    second = jnp.concatenate([above[HALO:], second_scene, below[HALO:]], axis=0)
    gathered = lax.all_gather(second, "strip", axis=0)
    first = jnp.concatenate([above[:HALO], first_scene, below[:HALO]], axis=0)
    before, after = both_ways("strip", first[:, -LANES:], first[:, :LANES])
    first = jnp.concatenate([before, first, after], axis=1)
    result = surfaces(
        first,
        gathered,
        owner_strip.reshape(patch_count),
        target_tile.reshape(patch_count),
        offsets.reshape(2 * patch_count),
        valid_mask.reshape(patch_count),
    )
    return result.reshape(1, 1, patch_count, SHIFTS * SHIFTS)


def solution(mesh):
    return jax.shard_map(
        on_device,
        mesh=mesh,
        in_specs=(
            P("band", "strip"),
            P("band", "strip"),
            P("band", "strip", None, None),
            P("band", "strip", None),
            P("band", "strip", None, None),
            P("band", "strip", None),
        ),
        out_specs=P("band", "strip", None, None),
        check_vma=False,
    )
```
